32 devices in a mesh: groups: 2 (over y), edge: 4 (over z), trip: 2 (over x), sub: 2 (over core).
Axes of the slice: x: 2, y: 2, z: 4, core: 2. Of those that a mesh axis runs over, the one named last changes fastest.
Arguments:
- edge_feat: float32 [128, 128, 512], P(('groups', 'edge'), ('trip', 'sub')), parts along dimension 0, may hold values from -6 to 6
- edge_counts: int32 [128], P(('groups', 'edge')), parts along dimension 0, may hold values from 64 to 128
- reverse: int32 [128], P('groups'), parts along dimension 0, may hold values from 0 to 63, as said below
- patterns: int32 [8, 4, 64, 2], P(('groups', 'edge'), ('trip', 'sub')), parts along dimension 0, may hold values from 0 to 15
- trip_count: int32 [8, 4], P(('groups', 'edge'), ('trip', 'sub')), parts along dimension 0, may hold values from 16 to 64, as said below
- coef: float32 [8, 4, 64, 128, 128], P(('groups', 'edge'), ('trip', 'sub')), parts along dimension 0, may hold values from -0.1875 to 0.1875
- down_weight: float32 [3, 512, 256], replicated, may hold values from -0.25 to 0.25
- up_weight: float32 [3, 256, 512], replicated, may hold values from -0.375 to 0.375
- dense_weight: float32 [3, 512, 512], replicated, may hold values from -0.25 to 0.25
Outputs:
- edge_out: float32 [128, 128, 512], P(('groups', 'edge'), ('trip', 'sub')), parts along dimension 0
The draws below stay inside these ranges and needn't reach their ends.
There are 2 independent parts, one for each index of `groups`. The reference program is written for one: setup_inputs(seed, part) draws one part's arguments, and reference() takes and returns one part's arrays. A program takes and returns all parts, laid end to end along the dimension named above; an argument that names none is the same for every part. Nothing has to cross between parts.
Inputs may be any that keep to these rules, and one draw needn't show every extreme that they name: reverse is an involution without fixed points; reverse[c] lies on another index of edge than c; from one index of edge at most 8 clusters have their reverse on one other index, and that many in every draw. `trip_count`: some device has all 64 slots live in every draw.
All inputs are finite; a program needn't handle non-finite values.
Results may differ from the reference program's by a relative error of at most 0.0003.
Values sent between devices are 32-bit elements; how exact they have to be, the bound alone decides.
A program may use at most 128 MiB of HBM per device.

```python
import jax
import jax.numpy as jnp
from jax import lax

DE = 512
FT = 256
BLK = 128
LAYERS = 3
EB = 16
P_SIZE = 64
GRID = 4
TS = 4
CLUSTERS = 64


def draw_reverse(key, part):
    keys = jax.random.split(jax.random.fold_in(key, 11), 2)
    place_perm = jax.random.permutation(keys[0], GRID).astype(jnp.int32)
    inverse_perm = jnp.zeros((GRID,), jnp.int32).at[place_perm].set(jnp.arange(GRID, dtype=jnp.int32))
    rounds = EB // 2
    round_ids = jnp.arange(rounds, dtype=jnp.int32)
    offsets = 2 * (round_ids % (GRID // 2)) + 1
    partner = inverse_perm[(offsets[None, :] - place_perm[:, None]) % GRID]
    slot_keys = jax.random.split(keys[1], GRID)
    slot_perms = jax.vmap(lambda sub_key: jax.random.permutation(sub_key, EB).astype(jnp.int32))(slot_keys)
    even_slot = slot_perms[:, 0::2]
    odd_slot = slot_perms[:, 1::2]
    partner_even = slot_perms[partner, 2 * round_ids[None, :]]
    partner_odd = slot_perms[partner, 2 * round_ids[None, :] + 1]
    values_even = partner * EB + partner_odd
    values_odd = partner * EB + partner_even
    device_ids = jnp.arange(GRID, dtype=jnp.int32)[:, None]
    result = jnp.zeros((GRID, EB), jnp.int32)
    result = result.at[device_ids, even_slot].set(values_even)
    result = result.at[device_ids, odd_slot].set(values_odd)
    return result.reshape(CLUSTERS).astype(jnp.int32)


def draw_edge_counts(key, part):
    keys = jax.random.split(jax.random.fold_in(key, 23), 3)
    counts = jax.random.randint(keys[0], (CLUSTERS,), BLK // 2, BLK + 1).astype(jnp.int32)
    first = jax.random.randint(keys[1], (), 0, CLUSTERS)
    second = (first + 1 + jax.random.randint(keys[2], (), 0, CLUSTERS - 1)) % CLUSTERS
    counts = counts.at[first].set(BLK).at[second].set(BLK // 2)
    return counts.astype(jnp.int32)


def draw_trip_count(key, part):
    keys = jax.random.split(jax.random.fold_in(key, 37), 2)
    counts = jax.random.randint(keys[0], (GRID * TS,), P_SIZE // 4, P_SIZE + 1).astype(jnp.int32)
    chosen = jax.random.randint(keys[1], (), 0, GRID * TS)
    counts = counts.at[chosen].set(P_SIZE)
    return counts.reshape(GRID, TS).astype(jnp.int32)


def touch_ends(values, stream_key, low, largest):
    place = [jax.random.randint(jax.random.fold_in(stream_key, axis), (), 0, length) for axis, length in enumerate(values.shape)]
    main_axis = values.shape.index(max(values.shape))
    beside = place[:main_axis] + [(place[main_axis] + 1) % values.shape[main_axis]] + place[main_axis + 1:]
    return values.at[tuple(place)].set(low).at[tuple(beside)].set(largest)


def shard_levels(rng, shape, pieces, smallest, top_value):
    def one(axis_at, shards_of):
        heights = jax.random.uniform(jax.random.fold_in(jax.random.fold_in(rng, 6), axis_at), (shards_of,), jnp.float32, smallest / len(pieces), top_value / len(pieces))
        return jnp.repeat(jnp.exp(heights), shape[axis_at] // shards_of).reshape((-1,) + (1,) * (len(shape) - axis_at - 1))

    loudness = one(*pieces[0])
    for cut in pieces[1:]:
        loudness = loudness * one(*cut)
    return loudness


def bell_draw(rng, shape, scale, reach, pieces=(), kind=jnp.bfloat16):
    factor_of = shard_levels(rng, shape, pieces, -0.22, 0.18) if pieces else 1.0
    values = jax.random.normal(rng, shape, jnp.float32) * scale * factor_of
    return jnp.minimum(jnp.maximum(values, -reach), reach).astype(kind)


def setup_inputs(seed: int = 0, part: int = 0) -> dict:
    key_of = jax.random.split(jax.random.key(seed), 10)
    part_keys = jax.random.split(jax.random.fold_in(key_of[9], part), 10)
    return {
        "edge_feat": bell_draw(part_keys[0], (CLUSTERS, BLK, DE), 1.0, 6.0, ((0, 4), (1, 4)), jnp.float32),
        "edge_counts": draw_edge_counts(jax.random.fold_in(jax.random.fold_in(key_of[9], part), 71), part),
        "reverse": draw_reverse(jax.random.fold_in(jax.random.fold_in(key_of[9], part), 71), part),
        "patterns": touch_ends(jax.random.randint(part_keys[3], (GRID, TS, P_SIZE, 2), 0, EB), jax.random.fold_in(part_keys[3], 1), 0, EB - 1).astype(jnp.int32),
        "trip_count": draw_trip_count(jax.random.fold_in(jax.random.fold_in(key_of[9], part), 71), part),
        "coef": bell_draw(part_keys[5], (GRID, TS, P_SIZE, BLK, BLK), (BLK * P_SIZE * TS // (2 * EB)) ** -0.5, 0.1875, ((0, 4), (1, 4)), jnp.float32),
        "down_weight": bell_draw(key_of[6], (LAYERS, DE, FT), DE ** -0.5, 0.25, (), jnp.float32),
        "up_weight": bell_draw(key_of[7], (LAYERS, FT, DE), FT ** -0.5, 0.375, (), jnp.float32),
        "dense_weight": bell_draw(key_of[8], (LAYERS, DE, DE), DE ** -0.5, 0.25, (), jnp.float32),
    }


EXACT_PRECISION = lax.Precision.HIGHEST
INV_THREE = 1.0 / 3.0 ** 0.5
INV_TWO = 1.0 / 2.0 ** 0.5


def reference(edge_feat, edge_counts, reverse, patterns, trip_count, coef, down_weight, up_weight, dense_weight):
    row_ids = jnp.arange(BLK, dtype=jnp.int32)
    valid_row_mask = (row_ids[None, :] < edge_counts[:, None]).astype(jnp.float32)[:, :, None]
    edge_features = edge_feat

    def per_group(inputs):
        group_blocks, pattern_list, live_count, coeffs = inputs
        slot_live = (jnp.arange(P_SIZE, dtype=jnp.int32)[None, :] < live_count[:, None]).astype(jnp.float32)
        flat_pattern = pattern_list.reshape(TS * P_SIZE, 2)
        flat_coeffs = coeffs.reshape(TS * P_SIZE, BLK, BLK)
        picked = jnp.take(group_blocks, flat_pattern[:, 1], axis=0)
        products = jnp.einsum('pij,pjf->pif', flat_coeffs, picked, precision=EXACT_PRECISION)
        products = products * slot_live.reshape(TS * P_SIZE)[:, None, None]
        target_hot = (flat_pattern[:, 0][None, :] == jnp.arange(EB, dtype=jnp.int32)[:, None]).astype(jnp.float32)
        return jnp.einsum('tp,pif->tif', target_hot, products, precision=EXACT_PRECISION)

    for current_layer_index in range(LAYERS):
        reduced_features = jnp.einsum('mrv,ve->mre', edge_features, down_weight[current_layer_index], precision=EXACT_PRECISION) * valid_row_mask
        grouped = reduced_features.reshape(GRID, EB, BLK, FT)
        pooled_messages = lax.map(per_group, (grouped, patterns, trip_count, coef)).reshape(CLUSTERS, BLK, FT)
        raised_features = jnp.einsum('dhi,iw->dhw', pooled_messages, up_weight[current_layer_index], precision=EXACT_PRECISION)
        reversed_feat = jnp.take(raised_features, reverse, axis=0)
        merged_features = (edge_features + raised_features + reversed_feat) * INV_THREE
        dense_output = jnp.einsum('weo,oa->wea', merged_features, dense_weight[current_layer_index], precision=EXACT_PRECISION)
        edge_features = (merged_features + jax.nn.silu(dense_output)) * INV_TWO
    return edge_features
```

```python
import jax
import jax.numpy as jnp
from jax import lax
from jax.sharding import PartitionSpec as P

EXACT_PRECISION = lax.Precision.HIGH
INV_THREE = 1.0 / 3.0**0.5
INV_TWO = 1.0 / 2.0**0.5


def local(
    edge_feat,
    edge_counts,
    reverse,
    patterns,
    trip_count,
    coef,
    down_weight,
    up_weight,
    dense_weight,
):
    block_count, row_share, feat_width = edge_feat.shape
    edge_size = lax.axis_size("edge")
    trip_rank = lax.axis_index(("trip", "sub"))
    edge_rank = lax.axis_index("edge")
    slot_cap = 2 * ((block_count // 2 + edge_size // 2 - 1) // (edge_size // 2))
    total_slots = edge_size * slot_cap
    all_clusters = reverse.shape[0]
    row_ids = trip_rank * row_share + jnp.arange(row_share, dtype=jnp.int32)
    valid_row_mask = (row_ids[None, :] < edge_counts[:, None]).astype(jnp.float32)[:, :, None]
    pattern_list = patterns[0, 0]
    live_count = trip_count[0, 0]
    coeffs = coef[0, 0]
    pattern_slots = pattern_list.shape[0]
    slot_live = (jnp.arange(pattern_slots, dtype=jnp.int32) < live_count).astype(jnp.float32)
    local_ids = jnp.arange(block_count, dtype=jnp.int32)
    target_hot = (pattern_list[:, 0][None, :] == local_ids[:, None]).astype(jnp.float32)
    mine_reverse = lax.dynamic_slice_in_dim(reverse, edge_rank * block_count, block_count)
    target_dev = mine_reverse // block_count
    same_target = target_dev[:, None] == target_dev[None, :]
    earlier_slot = local_ids[None, :] < local_ids[:, None]
    send_slot = jnp.sum((same_target & earlier_slot).astype(jnp.int32), axis=1)
    send_pos = target_dev * slot_cap + send_slot
    slot_ids = jnp.arange(total_slots, dtype=jnp.int32)
    send_hot = (slot_ids[:, None] == send_pos[None, :]).astype(jnp.float32)
    source_dev = mine_reverse // block_count
    all_dest = reverse // block_count
    cluster_ids = jnp.arange(all_clusters, dtype=jnp.int32)
    matches = (
        (cluster_ids[None, :] // block_count == source_dev[:, None])
        & (cluster_ids[None, :] < mine_reverse[:, None])
        & (all_dest[None, :] == edge_rank)
    )
    recv_slot = jnp.sum(matches.astype(jnp.int32), axis=1)
    recv_pos = source_dev * slot_cap + recv_slot
    recv_hot = (recv_pos[:, None] == slot_ids[None, :]).astype(jnp.float32)
    edge_features = edge_feat
    for current_layer_index in range(down_weight.shape[0]):
        reduced_features = (
            jnp.einsum(
                "mrv,ve->mre",
                edge_features,
                down_weight[current_layer_index],
                precision=EXACT_PRECISION,
            )
            * valid_row_mask
        )
        gathered = lax.all_gather(reduced_features, ("trip", "sub"), axis=1, tiled=True)
        picked = jnp.take(gathered, pattern_list[:, 1], axis=0)
        products = (
            jnp.einsum("pij,pjf->pif", coeffs, picked, precision=EXACT_PRECISION)
            * slot_live[:, None, None]
        )
        partials = jnp.einsum("tp,pif->tif", target_hot, products, precision=EXACT_PRECISION)
        pooled_messages = lax.psum_scatter(partials, ("trip", "sub"), scatter_dimension=1, tiled=True)
        narrow = pooled_messages.shape[2]
        packed = jnp.einsum(
            "kq,qrg->krg", send_hot, pooled_messages, precision=EXACT_PRECISION
        ).reshape(edge_size, slot_cap, row_share, narrow)
        arrived = lax.all_to_all(packed, "edge", split_axis=0, concat_axis=0, tiled=True)
        moved_rows = jnp.einsum(
            "qk,krg->qrg",
            recv_hot,
            arrived.reshape(total_slots, row_share, narrow),
            precision=EXACT_PRECISION,
        )
        raised_features = jnp.einsum(
            "dhi,iw->dhw",
            pooled_messages + moved_rows,
            up_weight[current_layer_index],
            precision=EXACT_PRECISION,
        )
        merged_features = (edge_features + raised_features) * INV_THREE
        dense_output = jnp.einsum(
            "weo,oa->wea",
            merged_features,
            dense_weight[current_layer_index],
            precision=EXACT_PRECISION,
        )
        edge_features = (merged_features + jax.nn.silu(dense_output)) * INV_TWO
    return edge_features


def solution(mesh):
    placed = (
        P(("groups", "edge"), ("trip", "sub"), None),
        P(("groups", "edge")),
        P("groups"),
        P(("groups", "edge"), ("trip", "sub"), None, None),
        P(("groups", "edge"), ("trip", "sub")),
        P(("groups", "edge"), ("trip", "sub"), None, None, None),
        P(),
        P(),
        P(),
    )
    return jax.shard_map(
        local,
        mesh=mesh,
        in_specs=placed,
        out_specs=P(("groups", "edge"), ("trip", "sub"), None),
        check_vma=False,
    )
```

```python
import functools

import jax
import jax.numpy as jnp
from jax import lax
from jax.experimental import pallas as pl
from jax.experimental.pallas import tpu as pltpu
from jax.sharding import PartitionSpec as P

INV_THREE = 1.0 / 3.0**0.5
INV_TWO = 1.0 / 2.0**0.5
F32, BF16 = jnp.float32, jnp.bfloat16
MESH = pl.DeviceIdType.MESH
CHUNK = 8


def split(x):
    hi = x.astype(BF16)
    return hi, (x - hi.astype(F32)).astype(BF16)


def dot(a, b):
    return jnp.dot(a, b, preferred_element_type=F32)


def mm3(x, w_hi, w_lo):
    rows = x.shape[0]
    hi, lo = split(x)
    both = dot(jnp.concatenate([hi, lo], axis=0), w_hi)
    return both[:rows] + both[rows:] + dot(hi, w_lo)


def kernel(dims, tab, mask, feat_hbm, coef_hbm, down_hbm, up_hbm, dense_hbm, out, *scratch):
    nt, ns, ne, eb, r, cap, slots, layers, blk, ft, de = dims
    nk, ranks = r // CHUNK, nt * ns
    zr, scratch = scratch[:nk], scratch[nk:]
    (coef, down, up, dense, down_h, down_l, up_h, up_l, dense_h, dense_l, c3, x3, run, part, recv1, recv2, agg, zs, gath,
     in_sem, agx_s, agp_s, agf_s, ag_r, r1_s, r1_r, r2_s, r2_r, z_s, z_r, z_free) = scratch
    o_perm, o_src, o_same = 0, slots, 2 * slots
    o_last, o_has = 3 * slots, 3 * slots + eb
    o_zsrc = o_has + eb
    o_zpos = o_zsrc + ne * cap
    a, b, e = lax.axis_index("trip"), lax.axis_index("sub"), lax.axis_index("edge")
    other = lax.rem(b + 1, ns)
    me = a * ns + b

    loads = [
        pltpu.make_async_copy(s, d, in_sem.at[i])
        for i, (s, d) in enumerate(((feat_hbm, out), (down_hbm, down), (coef_hbm, coef), (up_hbm, up), (dense_hbm, dense)))
    ]
    for load in loads:
        load.start()

    barrier = pltpu.get_barrier_semaphore()
    for o in range(1, nt):
        pl.semaphore_signal(barrier, inc=1, device_id={"trip": lax.rem(a + o, nt)}, device_id_type=MESH)
    pl.semaphore_signal(barrier, inc=1, device_id={"sub": other}, device_id_type=MESH)
    for o in range(1, ne):
        pl.semaphore_signal(barrier, inc=1, device_id={"edge": lax.rem(e + o, ne)}, device_id_type=MESH)

    def rows(k):
        return pl.ds(k * CHUNK, CHUNK)

    def remote(src, dst, send, recv, where):
        return pltpu.make_async_remote_copy(
            src_ref=src, dst_ref=dst, send_sem=send, recv_sem=recv, device_id=where, device_id_type=MESH
        )

    def ag_cross(k, o):
        g = gath.at[me, :, rows(k), :]
        return remote(g, g, agx_s.at[k, o], ag_r.at[k, me], {"trip": lax.rem(a + o, nt)})

    def ag_pair(k):
        g = gath.at[me, :, rows(k), :]
        return remote(g, g, agp_s.at[k], ag_r.at[k, me], {"sub": other})

    def ag_forward(k, o):
        rank = lax.rem(a + o, nt) * ns + b
        g = gath.at[rank, :, rows(k), :]
        return remote(g, g, agf_s.at[k, o], ag_r.at[k, rank], {"sub": other})

    def ag_arrive(k, rank):
        g = gath.at[rank, :, rows(k), :]
        remote(g, g, agp_s.at[k], ag_r.at[k, rank], {"sub": other}).wait_recv()

    def rs_pair(k):
        return remote(
            part.at[other, :, :, rows(k), :], recv1.at[:, :, rows(k), :], r1_s.at[k], r1_r.at[k], {"sub": other}
        )

    def rs_cross(k, o):
        peer = lax.rem(a + o, nt)
        return remote(
            part.at[b, peer, :, rows(k), :], recv2.at[a, :, rows(k), :], r2_s.at[k, o], r2_r.at[k, a], {"trip": peer}
        )

    def rs_arrive(k, o):
        src = lax.rem(a + o, nt)
        dst = recv2.at[src, :, rows(k), :]
        remote(dst, dst, r2_s.at[k, o], r2_r.at[k, src], {"trip": src}).wait_recv()

    def z_copy(k, o):
        peer = lax.rem(e + o, ne)
        return remote(
            zs.at[pl.ds(peer * cap, cap), rows(k), :],
            zr[k].at[pl.ds(e * cap, cap)],
            z_s.at[k, o],
            z_r.at[k, e],
            {"edge": peer},
        )

    def z_arrive(k, o):
        src = lax.rem(e + o, ne)
        dst = zr[k].at[pl.ds(src * cap, cap)]
        remote(dst, dst, z_s.at[k, o], z_r.at[k, src], {"edge": src}).wait_recv()

    def lower(k, layer):
        f = out[:, rows(k), :].reshape(eb * CHUNK, de)
        low = mm3(f, down_h[layer], down_l[layer]) * mask[k]
        gath[me, :, rows(k), :] = low.reshape(eb, CHUNK, ft)
        for o in range(1, nt):
            ag_cross(k, o).start()
        ag_pair(k).start()

    loads[1].wait()

    def split_down(i, _):
        hi, lo = split(down[i])
        down_h[i] = hi
        down_l[i] = lo
        return 0

    lax.fori_loop(0, layers, split_down, 0)
    loads[0].wait()
    pl.semaphore_wait(barrier, nt - 1 + 1 + ne - 1)
    for k in range(nk):
        lower(k, 0)
    loads[2].wait()

    def split_coef(p, _):
        hi, lo = split(coef[tab[o_perm + p]])
        c3[p, :, 0:blk] = hi
        c3[p, :, blk : 2 * blk] = lo
        c3[p, :, 2 * blk : 3 * blk] = hi
        return 0

    lax.fori_loop(0, slots, split_coef, 0)
    loads[3].wait()
    loads[4].wait()

    def split_rest(i, _):
        hi, lo = split(up[i])
        up_h[i] = hi
        up_l[i] = lo
        hi, lo = split(dense[i])
        dense_h[i] = hi
        dense_l[i] = lo
        return 0

    lax.fori_loop(0, layers, split_rest, 0)
    run[0] = jnp.zeros((blk, ft), F32)

    def layer_step(layer, _):
        for k in range(nk):
            for o in range(1, nt):
                ag_arrive(k, lax.rem(a + o, nt) * ns + b)
                ag_forward(k, o).start()
        for k in range(nk):
            for o in range(nt):
                ag_arrive(k, lax.rem(a + o, nt) * ns + other)
        for k in range(nk):
            ag_pair(k).wait_send()
            for o in range(1, nt):
                ag_cross(k, o).wait_send()
                ag_forward(k, o).wait_send()

        def widen(c, _):
            for rank in range(ranks):
                hi, lo = split(gath[rank, c])
                x3[c, rank * r : (rank + 1) * r, :] = hi
                x3[c, blk + rank * r : blk + (rank + 1) * r, :] = hi
                x3[c, 2 * blk + rank * r : 2 * blk + (rank + 1) * r, :] = lo
            return 0

        lax.fori_loop(0, eb, widen, 0)

        unroll = 4

        def triplets(i, _):
            for u in range(unroll):
                p = i * unroll + u
                keep = tab[o_same + p].astype(F32)
                run[p + 1] = run[p] * keep + dot(c3[p], x3[tab[o_src + p]])
            return 0

        lax.fori_loop(0, slots // unroll, triplets, 0)

        def collect(t, _):
            block = run[tab[o_last + t] + 1] * tab[o_has + t].astype(F32)
            for rank in range(ranks):
                part[rank % ns, rank // ns, t] = block[rank * r : (rank + 1) * r]
            return 0

        lax.fori_loop(0, eb, collect, 0)
        for k in range(nk):
            rs_pair(k).start()
        for k in range(nk):
            rs_pair(k).wait_recv()
            for o in range(1, nt):
                peer = lax.rem(a + o, nt)
                part[b, peer, :, rows(k), :] = part[b, peer, :, rows(k), :] + recv1[peer, :, rows(k), :]
                rs_cross(k, o).start()
            agg[:, rows(k), :] = part[b, a, :, rows(k), :] + recv1[a, :, rows(k), :]

        @pl.when(layer > 0)
        def _():
            pl.semaphore_wait(z_free, ne - 1)

        for k in range(nk):
            total = agg[:, rows(k), :]
            for o in range(1, nt):
                rs_arrive(k, o)
                total = total + recv2[lax.rem(a + o, nt), :, rows(k), :]
            agg[:, rows(k), :] = total
            for o in range(1, ne):
                base = lax.rem(e + o, ne) * cap
                for s in range(cap):
                    zs[base + s, rows(k), :] = agg[tab[o_zsrc + base + s], rows(k), :]
                z_copy(k, o).start()
        for k in range(nk):
            for o in range(1, ne):
                z_arrive(k, o)
            both = jnp.concatenate([agg[c, rows(k), :] + zr[k][tab[o_zpos + c]] for c in range(eb)], axis=0)
            lifted = mm3(both, up_h[layer], up_l[layer])
            f = out[:, rows(k), :].reshape(eb * CHUNK, de)
            mixed = (f + lifted) * INV_THREE
            v = mm3(mixed, dense_h[layer], dense_l[layer])
            new = (mixed + v / (1.0 + jnp.exp(-v))) * INV_TWO
            out[:, rows(k), :] = new.reshape(eb, CHUNK, de)

            @pl.when(layer + 1 < layers)
            def _():
                lower(k, layer + 1)

        @pl.when(layer + 1 < layers)
        def _():
            for o in range(1, ne):
                pl.semaphore_signal(z_free, inc=1, device_id={"edge": lax.rem(e + o, ne)}, device_id_type=MESH)

        for k in range(nk):
            rs_pair(k).wait_send()
            for o in range(1, nt):
                rs_cross(k, o).wait_send()
            for o in range(1, ne):
                z_copy(k, o).wait_send()
        return 0

    lax.fori_loop(0, layers, layer_step, 0)


def local(edge_feat, edge_counts, reverse, patterns, trip_count, coef, down_weight, up_weight, dense_weight):
    eb, r, de = edge_feat.shape
    nt, ns, ne = lax.axis_size("trip"), lax.axis_size("sub"), lax.axis_size("edge")
    layers, _, ft = down_weight.shape
    _, _, slots, blk, _ = coef.shape
    nk, ranks = r // CHUNK, nt * ns
    trip_rank = lax.axis_index(("trip", "sub"))
    edge_rank = lax.axis_index("edge")
    cap = 2 * ((eb // 2 + ne // 2 - 1) // (ne // 2))
    i32 = jnp.int32
    row_ids = trip_rank * r + jnp.arange(nk, dtype=i32)[:, None, None] * CHUNK + jnp.arange(CHUNK, dtype=i32)[None, None, :]
    mask = (row_ids < edge_counts[None, :, None]).astype(F32).reshape(nk, eb * CHUNK, 1)
    ids = jnp.arange(slots, dtype=i32)
    key = jnp.where(ids < trip_count[0, 0], patterns[0, 0, :, 0], eb)
    before = (key[None, :] < key[:, None]) | ((key[None, :] == key[:, None]) & (ids[None, :] < ids[:, None]))
    rank = jnp.sum(before.astype(i32), axis=1)
    hot = (rank[None, :] == ids[:, None]).astype(i32)
    perm = jnp.sum(hot * ids[None, :], axis=1)
    source = jnp.sum(hot * patterns[0, 0, :, 1][None, :], axis=1)
    first = jnp.sum((key[None, :] < key[:, None]).astype(i32), axis=1)
    same = jnp.sum(hot * (first < rank).astype(i32)[None, :], axis=1)
    cl = jnp.arange(eb, dtype=i32)
    upto = jnp.sum((key[None, :] <= cl[:, None]).astype(i32), axis=1)
    has = jnp.any(key[None, :] == cl[:, None], axis=1).astype(i32)
    last = jnp.maximum(upto - 1, 0)
    mine = lax.dynamic_slice_in_dim(reverse, edge_rank * eb, eb)
    dev = mine // eb
    send_slot = jnp.sum(((dev[:, None] == dev[None, :]) & (cl[None, :] < cl[:, None])).astype(i32), axis=1)
    zslots = jnp.arange(ne * cap, dtype=i32)
    zsrc = jnp.sum(jnp.where(zslots[:, None] == (dev * cap + send_slot)[None, :], cl[None, :], 0), axis=1)
    all_ids = jnp.arange(reverse.shape[0], dtype=i32)
    match = (
        (all_ids[None, :] // eb == dev[:, None])
        & (all_ids[None, :] < mine[:, None])
        & (reverse[None, :] // eb == edge_rank)
    )
    zpos = dev * cap + jnp.sum(match.astype(i32), axis=1)
    tab = jnp.concatenate([perm, source, same, last, has, zsrc, zpos]).astype(i32)

    dims = (nt, ns, ne, eb, r, cap, slots, layers, blk, ft, de)
    vm = pltpu.VMEM
    dma = pltpu.SemaphoreType.DMA
    scratch = [vm((ne * cap, CHUNK, ft), F32) for _ in range(nk)] + [
        vm((slots, blk, blk), F32),
        vm(down_weight.shape, F32),
        vm(up_weight.shape, F32),
        vm(dense_weight.shape, F32),
        vm(down_weight.shape, BF16),
        vm(down_weight.shape, BF16),
        vm(up_weight.shape, BF16),
        vm(up_weight.shape, BF16),
        vm(dense_weight.shape, BF16),
        vm(dense_weight.shape, BF16),
        vm((slots, blk, 3 * blk), BF16),
        vm((eb, 3 * blk, ft), BF16),
        vm((slots + 1, blk, ft), F32),
        vm((ns, nt, eb, r, ft), F32),
        vm((nt, eb, r, ft), F32),
        vm((nt, eb, r, ft), F32),
        vm((eb, r, ft), F32),
        vm((ne * cap, r, ft), F32),
        vm((ranks, eb, r, ft), F32),
        dma((5,)),
        dma((nk, nt)),
        dma((nk,)),
        dma((nk, nt)),
        dma((nk, ranks)),
        dma((nk,)),
        dma((nk,)),
        dma((nk, nt)),
        dma((nk, nt)),
        dma((nk, ne)),
        dma((nk, ne)),
        pltpu.SemaphoreType.REGULAR,
    ]
    anywhere = pl.BlockSpec(memory_space=pl.ANY)
    return pl.pallas_call(
        functools.partial(kernel, dims),
        out_shape=jax.ShapeDtypeStruct(edge_feat.shape, F32),
        in_specs=[pl.BlockSpec(memory_space=pltpu.SMEM), pl.BlockSpec(memory_space=pltpu.VMEM)] + [anywhere] * 5,
        out_specs=pl.BlockSpec(memory_space=pltpu.VMEM),
        scratch_shapes=scratch,
        compiler_params=pltpu.CompilerParams(collective_id=0, has_side_effects=True, vmem_limit_bytes=64 * 1024 * 1024 - 65536),
    )(tab, mask, edge_feat, coef[0, 0], down_weight, up_weight, dense_weight)


def solution(mesh):
    placed = (
        P(("groups", "edge"), ("trip", "sub"), None),
        P(("groups", "edge")),
        P("groups"),
        P(("groups", "edge"), ("trip", "sub"), None, None),
        P(("groups", "edge"), ("trip", "sub")),
        P(("groups", "edge"), ("trip", "sub"), None, None, None),
        P(),
        P(),
        P(),
    )
    return jax.shard_map(
        local,
        mesh=mesh,
        in_specs=placed,
        out_specs=P(("groups", "edge"), ("trip", "sub"), None),
        check_vma=False,
    )
```

```python
import functools

import jax
import jax.numpy as jnp
from jax import lax
from jax.experimental import pallas as pl
from jax.experimental.pallas import tpu as pltpu
from jax.sharding import PartitionSpec as P

INV_THREE = 1.0 / 3.0**0.5
INV_TWO = 1.0 / 2.0**0.5
F32, BF16 = jnp.float32, jnp.bfloat16
MESH = pl.DeviceIdType.MESH
CHUNK = 8


def split(x):
    hi = x.astype(BF16)
    return hi, (x - hi.astype(F32)).astype(BF16)


def dot(a, b):
    return jnp.dot(a, b, preferred_element_type=F32)


def mm3(x, w_hi, w_lo):
    rows = x.shape[0]
    hi, lo = split(x)
    both = dot(jnp.concatenate([hi, lo], axis=0), w_hi)
    return both[:rows] + both[rows:] + dot(hi, w_lo)


def kernel(dims, tab, feat_hbm, coef_hbm, down_hbm, up_hbm, dense_hbm, out, *scratch):
    nt, ns, ne, eb, r, cap, slots, layers, blk, ft, de = dims
    nk, ranks, half, wide = r // CHUNK, nt * ns, eb // 2, ft // 2
    zr, scratch = scratch[: 2 * nk], scratch[2 * nk :]
    (coef, down, up, dense, down_h, down_l, up_h, up_l, dense_h, dense_l, c3, x3, run, part, recv1, recv2, agg, zs, gath, mask,
     in_sem, agx_s, agp_s, agf_s, ag_r, r1_s, r1_r, r2_s, r2_r, z_s, z_r, z_free) = scratch
    o_perm, o_src, o_same = 0, slots, 2 * slots
    o_last, o_has = 3 * slots, 3 * slots + eb
    o_zsrc = o_has + eb
    o_zpos = o_zsrc + ne * cap
    o_count = o_zpos + eb
    a, b, e = lax.axis_index("trip"), lax.axis_index("sub"), lax.axis_index("edge")
    other = lax.rem(b + 1, ns)
    me = a * ns + b

    loads = [
        pltpu.make_async_copy(s, d, in_sem.at[i])
        for i, (s, d) in enumerate(((feat_hbm, out), (down_hbm, down), (coef_hbm, coef), (up_hbm, up), (dense_hbm, dense)))
    ]
    for load in loads:
        load.start()

    barrier = pltpu.get_barrier_semaphore()
    for o in range(1, nt):
        pl.semaphore_signal(barrier, inc=1, device_id={"trip": lax.rem(a + o, nt)}, device_id_type=MESH)
    pl.semaphore_signal(barrier, inc=1, device_id={"sub": other}, device_id_type=MESH)
    for o in range(1, ne):
        pl.semaphore_signal(barrier, inc=1, device_id={"edge": lax.rem(e + o, ne)}, device_id_type=MESH)

    def rows(k):
        return pl.ds(k * CHUNK, CHUNK)

    def remote(src, dst, send, recv, where):
        return pltpu.make_async_remote_copy(
            src_ref=src, dst_ref=dst, send_sem=send, recv_sem=recv, device_id=where, device_id_type=MESH
        )

    def cols(h):
        return pl.ds(h * wide, wide)

    def gather_piece(rank, k, h):
        return gath.at[rank, pl.ds(h * half, half), rows(k), :]

    def ag_cross(k, h, o):
        g = gather_piece(me, k, h)
        return remote(g, g, agx_s.at[2 * k + h, o], ag_r.at[2 * k + h, me], {"trip": lax.rem(a + o, nt)})

    def ag_pair(k, h):
        g = gather_piece(me, k, h)
        return remote(g, g, agp_s.at[2 * k + h], ag_r.at[2 * k + h, me], {"sub": other})

    def ag_forward(k, h, o):
        rank = lax.rem(a + o, nt) * ns + b
        g = gather_piece(rank, k, h)
        return remote(g, g, agf_s.at[2 * k + h, o], ag_r.at[2 * k + h, rank], {"sub": other})

    def ag_arrive(k, h, rank):
        g = gather_piece(rank, k, h)
        remote(g, g, agp_s.at[2 * k + h], ag_r.at[2 * k + h, rank], {"sub": other}).wait_recv()

    def pass_on(k):
        for h in range(2):
            for o in range(1, nt):
                ag_arrive(k, h, lax.rem(a + o, nt) * ns + b)
                ag_forward(k, h, o).start()

    def rs_pair(k, h):
        return remote(
            part.at[other, :, :, rows(k), cols(h)],
            recv1.at[:, :, rows(k), cols(h)],
            r1_s.at[2 * k + h],
            r1_r.at[2 * k + h],
            {"sub": other},
        )

    def rs_cross(k, h, o):
        peer = lax.rem(a + o, nt)
        return remote(
            part.at[b, peer, :, rows(k), cols(h)],
            recv2.at[a, :, rows(k), cols(h)],
            r2_s.at[2 * k + h, o],
            r2_r.at[2 * k + h, a],
            {"trip": peer},
        )

    def rs_arrive(k, h, o):
        src = lax.rem(a + o, nt)
        dst = recv2.at[src, :, rows(k), cols(h)]
        remote(dst, dst, r2_s.at[2 * k + h, o], r2_r.at[2 * k + h, src], {"trip": src}).wait_recv()

    def z_copy(k, h, o):
        peer = lax.rem(e + o, ne)
        return remote(
            zs.at[pl.ds(peer * cap, cap), rows(k), cols(h)],
            zr[2 * k + h].at[pl.ds(e * cap, cap)],
            z_s.at[2 * k + h, o],
            z_r.at[2 * k + h, e],
            {"edge": peer},
        )

    def z_arrive(k, h, o):
        src = lax.rem(e + o, ne)
        dst = zr[2 * k + h].at[pl.ds(src * cap, cap)]
        remote(dst, dst, z_s.at[2 * k + h, o], z_r.at[2 * k + h, src], {"edge": src}).wait_recv()

    def lower(k, layer):
        for h in range(2):
            f = out[h * half : (h + 1) * half, rows(k), :].reshape(half * CHUNK, de)
            live = jnp.concatenate([mask[k, h * half * CHUNK : (h + 1) * half * CHUNK, :]] * (ft // 128), axis=1)
            low = mm3(f, down_h[layer], down_l[layer]) * live
            gath[me, h * half : (h + 1) * half, rows(k), :] = low.reshape(half, CHUNK, ft)
            for o in range(1, nt):
                ag_cross(k, h, o).start()
            ag_pair(k, h).start()

    for k in range(nk):
        ids = me * r + k * CHUNK + lax.broadcasted_iota(jnp.int32, (CHUNK, 128), 0)
        for c in range(eb):
            mask[k, c * CHUNK : (c + 1) * CHUNK, :] = jnp.where(ids < tab[o_count + c], 1.0, 0.0).astype(F32)
    loads[1].wait()

    def split_down(i, _):
        hi, lo = split(down[i])
        down_h[i] = hi
        down_l[i] = lo
        return 0

    lax.fori_loop(0, layers, split_down, 0)
    loads[0].wait()
    pl.semaphore_wait(barrier, nt - 1 + 1 + ne - 1)
    for k in range(nk):
        lower(k, 0)
    loads[2].wait()

    def split_coef(p, _):
        hi, lo = split(coef[tab[o_perm + p]])
        c3[p, :, 0:blk] = hi
        c3[p, :, blk : 2 * blk] = lo
        c3[p, :, 2 * blk : 3 * blk] = hi
        return 0

    lax.fori_loop(0, slots, split_coef, 0)
    loads[3].wait()
    loads[4].wait()

    def split_rest(i, _):
        hi, lo = split(up[i])
        up_h[i] = hi
        up_l[i] = lo
        hi, lo = split(dense[i])
        dense_h[i] = hi
        dense_l[i] = lo
        return 0

    lax.fori_loop(0, layers, split_rest, 0)
    run[0] = jnp.zeros((blk, ft), F32)
    for k in range(nk - 2):
        pass_on(k)

    def layer_step(layer, _):
        for k in range(max(nk - 2, 0), nk):
            pass_on(k)

        def widen(first):
            def step(c, _):
                for rank in range(ranks):
                    hi, lo = split(gath[rank, c, first : first + 2 * CHUNK, :])
                    at = rank * r + first
                    x3[c, at : at + 2 * CHUNK, :] = hi
                    x3[c, blk + at : blk + at + 2 * CHUNK, :] = hi
                    x3[c, 2 * blk + at : 2 * blk + at + 2 * CHUNK, :] = lo
                return 0

            lax.fori_loop(0, eb, step, 0)

        for pair in range(nk // 2):
            for k in (2 * pair, 2 * pair + 1):
                for h in range(2):
                    for o in range(nt):
                        ag_arrive(k, h, lax.rem(a + o, nt) * ns + other)
            widen(2 * pair * CHUNK)
        for k in range(nk):
            for h in range(2):
                ag_pair(k, h).wait_send()
                for o in range(1, nt):
                    ag_cross(k, h, o).wait_send()
                    ag_forward(k, h, o).wait_send()

        unroll = 16

        def triplets(i, _):
            for u in range(unroll):
                p = i * unroll + u
                keep = tab[o_same + p].astype(F32)
                run[p + 1] = run[p] * keep + dot(c3[p], x3[tab[o_src + p]])
            return 0

        lax.fori_loop(0, slots // unroll, triplets, 0)

        for k in range(nk):

            def collect(t, _):
                at, has = tab[o_last + t] + 1, tab[o_has + t].astype(F32)
                for rank in range(ranks):
                    first = rank * r + k * CHUNK
                    part[rank % ns, rank // ns, t, rows(k), :] = run[at, first : first + CHUNK, :] * has
                return 0

            lax.fori_loop(0, eb, collect, 0)
            for h in range(2):
                rs_pair(k, h).start()
        for k in range(nk):
            for h in range(2):
                rs_pair(k, h).wait_recv()
                for o in range(1, nt):
                    peer = lax.rem(a + o, nt)
                    part[b, peer, :, rows(k), cols(h)] = (
                        part[b, peer, :, rows(k), cols(h)] + recv1[peer, :, rows(k), cols(h)]
                    )
                    rs_cross(k, h, o).start()
                agg[:, rows(k), cols(h)] = part[b, a, :, rows(k), cols(h)] + recv1[a, :, rows(k), cols(h)]

        @pl.when(layer > 0)
        def _():
            pl.semaphore_wait(z_free, ne - 1)

        for k in range(nk):
            for h in range(2):
                total = agg[:, rows(k), cols(h)]
                for o in range(1, nt):
                    rs_arrive(k, h, o)
                    total = total + recv2[lax.rem(a + o, nt), :, rows(k), cols(h)]
                agg[:, rows(k), cols(h)] = total
                for o in range(1, ne):
                    base = lax.rem(e + o, ne) * cap
                    for s in range(cap):
                        zs[base + s, rows(k), cols(h)] = agg[tab[o_zsrc + base + s], rows(k), cols(h)]
                    z_copy(k, h, o).start()
        for k in range(nk):
            sides = []
            for h in range(2):
                for o in range(1, ne):
                    z_arrive(k, h, o)
                sides.append(
                    jnp.concatenate(
                        [agg[c, rows(k), cols(h)] + zr[2 * k + h][tab[o_zpos + c]] for c in range(eb)], axis=0
                    )
                )
            both = jnp.concatenate(sides, axis=1)
            lifted = mm3(both, up_h[layer], up_l[layer])
            f = out[:, rows(k), :].reshape(eb * CHUNK, de)
            mixed = (f + lifted) * INV_THREE
            v = mm3(mixed, dense_h[layer], dense_l[layer])
            new = (mixed + v / (1.0 + jnp.exp(-v))) * INV_TWO
            out[:, rows(k), :] = new.reshape(eb, CHUNK, de)

            @pl.when(layer + 1 < layers)
            def _():
                lower(k, layer + 1)
                if k >= 2:
                    pass_on(k - 2)

        @pl.when(layer + 1 < layers)
        def _():
            for o in range(1, ne):
                pl.semaphore_signal(z_free, inc=1, device_id={"edge": lax.rem(e + o, ne)}, device_id_type=MESH)

        for k in range(nk):
            for h in range(2):
                rs_pair(k, h).wait_send()
                for o in range(1, nt):
                    rs_cross(k, h, o).wait_send()
                for o in range(1, ne):
                    z_copy(k, h, o).wait_send()
        return 0

    lax.fori_loop(0, layers, layer_step, 0)


def local(edge_feat, edge_counts, reverse, patterns, trip_count, coef, down_weight, up_weight, dense_weight):
    eb, r, de = edge_feat.shape
    nt, ns, ne = lax.axis_size("trip"), lax.axis_size("sub"), lax.axis_size("edge")
    layers, _, ft = down_weight.shape
    _, _, slots, blk, _ = coef.shape
    nk, ranks = r // CHUNK, nt * ns
    edge_rank = lax.axis_index("edge")
    cap = 2 * ((eb // 2 + ne // 2 - 1) // (ne // 2))
    i32 = jnp.int32
    ids = jnp.arange(slots, dtype=i32)
    key = jnp.where(ids < trip_count[0, 0], patterns[0, 0, :, 0], eb)
    before = (key[None, :] < key[:, None]) | ((key[None, :] == key[:, None]) & (ids[None, :] < ids[:, None]))
    rank = jnp.sum(before.astype(i32), axis=1)
    hot = (rank[None, :] == ids[:, None]).astype(i32)
    perm = jnp.sum(hot * ids[None, :], axis=1)
    source = jnp.sum(hot * patterns[0, 0, :, 1][None, :], axis=1)
    first = jnp.sum((key[None, :] < key[:, None]).astype(i32), axis=1)
    same = jnp.sum(hot * (first < rank).astype(i32)[None, :], axis=1)
    cl = jnp.arange(eb, dtype=i32)
    upto = jnp.sum((key[None, :] <= cl[:, None]).astype(i32), axis=1)
    has = jnp.any(key[None, :] == cl[:, None], axis=1).astype(i32)
    last = jnp.maximum(upto - 1, 0)
    mine = lax.dynamic_slice_in_dim(reverse, edge_rank * eb, eb)
    dev = mine // eb
    send_slot = jnp.sum(((dev[:, None] == dev[None, :]) & (cl[None, :] < cl[:, None])).astype(i32), axis=1)
    zslots = jnp.arange(ne * cap, dtype=i32)
    zsrc = jnp.sum(jnp.where(zslots[:, None] == (dev * cap + send_slot)[None, :], cl[None, :], 0), axis=1)
    all_ids = jnp.arange(reverse.shape[0], dtype=i32)
    match = (
        (all_ids[None, :] // eb == dev[:, None])
        & (all_ids[None, :] < mine[:, None])
        & (reverse[None, :] // eb == edge_rank)
    )
    zpos = dev * cap + jnp.sum(match.astype(i32), axis=1)
    tab = jnp.concatenate([perm, source, same, last, has, zsrc, zpos, edge_counts]).astype(i32)

    dims = (nt, ns, ne, eb, r, cap, slots, layers, blk, ft, de)
    vm = pltpu.VMEM
    dma = pltpu.SemaphoreType.DMA
    scratch = [vm((ne * cap, CHUNK, ft // 2), F32) for _ in range(2 * nk)] + [
        vm((slots, blk, blk), F32),
        vm(down_weight.shape, F32),
        vm(up_weight.shape, F32),
        vm(dense_weight.shape, F32),
        vm(down_weight.shape, BF16),
        vm(down_weight.shape, BF16),
        vm(up_weight.shape, BF16),
        vm(up_weight.shape, BF16),
        vm(dense_weight.shape, BF16),
        vm(dense_weight.shape, BF16),
        vm((slots, blk, 3 * blk), BF16),
        vm((eb, 3 * blk, ft), BF16),
        vm((slots + 1, blk, ft), F32),
        vm((ns, nt, eb, r, ft), F32),
        vm((nt, eb, r, ft), F32),
        vm((nt, eb, r, ft), F32),
        vm((eb, r, ft), F32),
        vm((ne * cap, r, ft), F32),
        vm((ranks, eb, r, ft), F32),
        vm((nk, eb * CHUNK, 128), F32),
        dma((5,)),
        dma((2 * nk, nt)),
        dma((2 * nk,)),
        dma((2 * nk, nt)),
        dma((2 * nk, ranks)),
        dma((2 * nk,)),
        dma((2 * nk,)),
        dma((2 * nk, nt)),
        dma((2 * nk, nt)),
        dma((2 * nk, ne)),
        dma((2 * nk, ne)),
        pltpu.SemaphoreType.REGULAR,
    ]
    anywhere = pl.BlockSpec(memory_space=pl.ANY)
    return pl.pallas_call(
        functools.partial(kernel, dims),
        out_shape=jax.ShapeDtypeStruct(edge_feat.shape, F32),
        in_specs=[pl.BlockSpec(memory_space=pltpu.SMEM)] + [anywhere] * 5,
        out_specs=pl.BlockSpec(memory_space=pltpu.VMEM),
        scratch_shapes=scratch,
        compiler_params=pltpu.CompilerParams(collective_id=0, has_side_effects=True, vmem_limit_bytes=64 * 1024 * 1024 - 65536),
    )(tab, edge_feat, coef[0, 0], down_weight, up_weight, dense_weight)


def solution(mesh):
    placed = (
        P(("groups", "edge"), ("trip", "sub"), None),
        P(("groups", "edge")),
        P("groups"),
        P(("groups", "edge"), ("trip", "sub"), None, None),
        P(("groups", "edge"), ("trip", "sub")),
        P(("groups", "edge"), ("trip", "sub"), None, None, None),
        P(),
        P(),
        P(),
    )
    return jax.shard_map(
        local,
        mesh=mesh,
        in_specs=placed,
        out_specs=P(("groups", "edge"), ("trip", "sub"), None),
        check_vma=False,
    )
```

```python
import functools

import jax
import jax.numpy as jnp
from jax import lax
from jax.experimental import pallas as pl
from jax.experimental.pallas import tpu as pltpu
from jax.sharding import PartitionSpec as P

INV_THREE = 1.0 / 3.0**0.5
INV_TWO = 1.0 / 2.0**0.5
F32, BF16 = jnp.float32, jnp.bfloat16
MESH = pl.DeviceIdType.MESH
CHUNK = 8


def split(x):
    hi = x.astype(BF16)
    return hi, (x - hi.astype(F32)).astype(BF16)


def dot(a, b):
    return jnp.dot(a, b, preferred_element_type=F32)


def mm3(x, w_hi, w_lo):
    rows = x.shape[0]
    hi, lo = split(x)
    both = dot(jnp.concatenate([hi, lo], axis=0), w_hi)
    return both[:rows] + both[rows:] + dot(hi, w_lo)


def kernel(dims, tab, feat_hbm, coef_hbm, down_hbm, up_hbm, dense_hbm, out, *scratch):
    nt, ns, ne, eb, r, cap, slots, layers, blk, ft, de = dims
    nk, ranks, half, wide = r // CHUNK, nt * ns, eb // 2, ft // 2
    zr, scratch = scratch[: 2 * nk], scratch[2 * nk :]
    (coef, down, up, dense, down_h, down_l, up_h, up_l, dense_h, dense_l, c3, x3, run, part, recv1, recv2, agg, zs, gath, mask,
     in_sem, agx_s, agp_s, agf_s, ag_r, r1_s, r1_r, r2_s, r2_r, z_s, z_r, z_free) = scratch
    o_perm, o_src, o_same = 0, slots, 2 * slots
    o_last, o_has = 3 * slots, 3 * slots + eb
    o_zsrc = o_has + eb
    o_zpos = o_zsrc + ne * cap
    o_count = o_zpos + eb
    a, b, e = lax.axis_index("trip"), lax.axis_index("sub"), lax.axis_index("edge")
    other = lax.rem(b + 1, ns)
    me = a * ns + b

    rest = pl.ds(1, layers - 1)
    loads = [
        pltpu.make_async_copy(s, d, in_sem.at[i])
        for i, (s, d) in enumerate(((feat_hbm, out), (down_hbm.at[rest], down.at[rest]), (coef_hbm, coef), (up_hbm, up), (dense_hbm, dense), (down_hbm.at[0], down.at[0])))
    ]
    loads[5].start()
    loads[0].start()

    barrier = pltpu.get_barrier_semaphore()
    for o in range(1, nt):
        pl.semaphore_signal(barrier, inc=1, device_id={"trip": lax.rem(a + o, nt)}, device_id_type=MESH)
    pl.semaphore_signal(barrier, inc=1, device_id={"sub": other}, device_id_type=MESH)
    for o in range(1, ne):
        pl.semaphore_signal(barrier, inc=1, device_id={"edge": lax.rem(e + o, ne)}, device_id_type=MESH)

    def rows(k):
        return pl.ds(k * CHUNK, CHUNK)

    def remote(src, dst, send, recv, where):
        return pltpu.make_async_remote_copy(
            src_ref=src, dst_ref=dst, send_sem=send, recv_sem=recv, device_id=where, device_id_type=MESH
        )

    def cols(h):
        return pl.ds(h * wide, wide)

    def gather_piece(rank, k, h):
        return gath.at[rank, pl.ds(h * half, half), rows(k), :]

    def ag_cross(k, h, o):
        g = gather_piece(me, k, h)
        return remote(g, g, agx_s.at[2 * k + h, o], ag_r.at[2 * k + h, me], {"trip": lax.rem(a + o, nt)})

    def ag_pair(k, h):
        g = gather_piece(me, k, h)
        return remote(g, g, agp_s.at[2 * k + h], ag_r.at[2 * k + h, me], {"sub": other})

    def ag_forward(k, h, o):
        rank = lax.rem(a + o, nt) * ns + b
        g = gather_piece(rank, k, h)
        return remote(g, g, agf_s.at[2 * k + h, o], ag_r.at[2 * k + h, rank], {"sub": other})

    def ag_arrive(k, h, rank):
        g = gather_piece(rank, k, h)
        remote(g, g, agp_s.at[2 * k + h], ag_r.at[2 * k + h, rank], {"sub": other}).wait_recv()

    def pass_on(k):
        for h in range(2):
            for o in range(1, nt):
                ag_arrive(k, h, lax.rem(a + o, nt) * ns + b)
                ag_forward(k, h, o).start()

    def rs_pair(k, h):
        return remote(
            part.at[other, :, :, rows(k), cols(h)],
            recv1.at[:, :, rows(k), cols(h)],
            r1_s.at[2 * k + h],
            r1_r.at[2 * k + h],
            {"sub": other},
        )

    def rs_cross(k, h, o):
        peer = lax.rem(a + o, nt)
        return remote(
            part.at[b, peer, :, rows(k), cols(h)],
            recv2.at[a, :, rows(k), cols(h)],
            r2_s.at[2 * k + h, o],
            r2_r.at[2 * k + h, a],
            {"trip": peer},
        )

    def rs_arrive(k, h, o):
        src = lax.rem(a + o, nt)
        dst = recv2.at[src, :, rows(k), cols(h)]
        remote(dst, dst, r2_s.at[2 * k + h, o], r2_r.at[2 * k + h, src], {"trip": src}).wait_recv()

    def z_copy(k, h, o):
        peer = lax.rem(e + o, ne)
        return remote(
            zs.at[pl.ds(peer * cap, cap), rows(k), cols(h)],
            zr[2 * k + h].at[pl.ds(e * cap, cap)],
            z_s.at[2 * k + h, o],
            z_r.at[2 * k + h, e],
            {"edge": peer},
        )

    def z_arrive(k, h, o):
        src = lax.rem(e + o, ne)
        dst = zr[2 * k + h].at[pl.ds(src * cap, cap)]
        remote(dst, dst, z_s.at[2 * k + h, o], z_r.at[2 * k + h, src], {"edge": src}).wait_recv()

    def lower(k, layer):
        for h in range(2):
            f = out[h * half : (h + 1) * half, rows(k), :].reshape(half * CHUNK, de)
            live = jnp.concatenate([mask[k, h * half * CHUNK : (h + 1) * half * CHUNK, :]] * (ft // 128), axis=1)
            low = mm3(f, down_h[layer], down_l[layer]) * live
            gath[me, h * half : (h + 1) * half, rows(k), :] = low.reshape(half, CHUNK, ft)
            for o in range(1, nt):
                ag_cross(k, h, o).start()
            ag_pair(k, h).start()

    for k in range(nk):
        ids = me * r + k * CHUNK + lax.broadcasted_iota(jnp.int32, (CHUNK, 128), 0)
        for c in range(eb):
            mask[k, c * CHUNK : (c + 1) * CHUNK, :] = jnp.where(ids < tab[o_count + c], 1.0, 0.0).astype(F32)
    loads[5].wait()
    loads[0].wait()
    for i in (2, 3, 4, 1):
        loads[i].start()

    def split_down(i, _):
        hi, lo = split(down[i])
        down_h[i] = hi
        down_l[i] = lo
        return 0

    split_down(0, 0)
    pl.semaphore_wait(barrier, nt - 1 + 1 + ne - 1)
    for k in range(nk):
        lower(k, 0)
    loads[2].wait()

    def split_coef(p, _):
        hi, lo = split(coef[tab[o_perm + p]])
        c3[p, :, 0:blk] = hi
        c3[p, :, blk : 2 * blk] = lo
        c3[p, :, 2 * blk : 3 * blk] = hi
        return 0

    lax.fori_loop(0, slots, split_coef, 0)
    for i in (3, 4, 1):
        loads[i].wait()
    lax.fori_loop(1, layers, split_down, 0)

    def split_rest(i, _):
        hi, lo = split(up[i])
        up_h[i] = hi
        up_l[i] = lo
        hi, lo = split(dense[i])
        dense_h[i] = hi
        dense_l[i] = lo
        return 0

    lax.fori_loop(0, layers, split_rest, 0)
    run[0] = jnp.zeros((blk, ft), F32)
    for k in range(nk - 2):
        pass_on(k)

    def layer_step(layer, _):
        if nk > 2:
            pass_on(nk - 2)

        def widen(first):
            def step(c, _):
                for rank in range(ranks):
                    hi, lo = split(gath[rank, c, first : first + 2 * CHUNK, :])
                    at = rank * r + first
                    x3[c, at : at + 2 * CHUNK, :] = hi
                    x3[c, blk + at : blk + at + 2 * CHUNK, :] = hi
                    x3[c, 2 * blk + at : 2 * blk + at + 2 * CHUNK, :] = lo
                return 0

            lax.fori_loop(0, eb, step, 0, unroll=4)

        for pair in range(nk // 2):
            if pair == nk // 2 - 1:
                for k in range(nk - 1 if nk > 2 else 0, nk):
                    pass_on(k)
            for k in (2 * pair, 2 * pair + 1):
                for h in range(2):
                    for o in range(nt):
                        ag_arrive(k, h, lax.rem(a + o, nt) * ns + other)
            widen(2 * pair * CHUNK)
        for k in range(nk):
            for h in range(2):
                ag_pair(k, h).wait_send()
                for o in range(1, nt):
                    ag_cross(k, h, o).wait_send()
                    ag_forward(k, h, o).wait_send()

        unroll = 16

        def triplets(i, _):
            for u in range(unroll):
                p = i * unroll + u
                keep = tab[o_same + p].astype(F32)
                run[p + 1] = run[p] * keep + dot(c3[p], x3[tab[o_src + p]])
            return 0

        lax.fori_loop(0, slots // unroll, triplets, 0)

        def cross(k):
            for h in range(2):
                rs_pair(k, h).wait_recv()
                for o in range(1, nt):
                    peer = lax.rem(a + o, nt)
                    part[b, peer, :, rows(k), cols(h)] = (
                        part[b, peer, :, rows(k), cols(h)] + recv1[peer, :, rows(k), cols(h)]
                    )
                    rs_cross(k, h, o).start()
                agg[:, rows(k), cols(h)] = part[b, a, :, rows(k), cols(h)] + recv1[a, :, rows(k), cols(h)]

        for k in range(nk):

            def collect(t, _):
                at, has = tab[o_last + t] + 1, tab[o_has + t].astype(F32)
                for rank in range(ranks):
                    first = rank * r + k * CHUNK
                    part[rank % ns, rank // ns, t, rows(k), :] = run[at, first : first + CHUNK, :] * has
                return 0

            lax.fori_loop(0, eb, collect, 0, unroll=4)
            for h in range(2):
                rs_pair(k, h).start()
            if k > 0:
                cross(k - 1)
        cross(nk - 1)

        @pl.when(layer > 0)
        def _():
            pl.semaphore_wait(z_free, ne - 1)

        for k in range(nk):
            for h in range(2):
                total = agg[:, rows(k), cols(h)]
                for o in range(1, nt):
                    rs_arrive(k, h, o)
                    total = total + recv2[lax.rem(a + o, nt), :, rows(k), cols(h)]
                agg[:, rows(k), cols(h)] = total
                for o in range(1, ne):
                    base = lax.rem(e + o, ne) * cap
                    for s in range(cap):
                        zs[base + s, rows(k), cols(h)] = agg[tab[o_zsrc + base + s], rows(k), cols(h)]
                    z_copy(k, h, o).start()
        for k in range(nk):
            sides = []
            for h in range(2):
                for o in range(1, ne):
                    z_arrive(k, h, o)
                sides.append(
                    jnp.concatenate(
                        [agg[c, rows(k), cols(h)] + zr[2 * k + h][tab[o_zpos + c]] for c in range(eb)], axis=0
                    )
                )
            both = jnp.concatenate(sides, axis=1)
            lifted = mm3(both, up_h[layer], up_l[layer])
            f = out[:, rows(k), :].reshape(eb * CHUNK, de)
            mixed = (f + lifted) * INV_THREE
            v = mm3(mixed, dense_h[layer], dense_l[layer])
            new = (mixed + v / (1.0 + jnp.exp(-v))) * jnp.where(layer + 1 < layers, INV_TWO, 1.0)
            out[:, rows(k), :] = new.reshape(eb, CHUNK, de)

            @pl.when(layer + 1 < layers)
            def _():
                lower(k, layer + 1)
                if k >= 2:
                    pass_on(k - 2)

        @pl.when(layer + 1 < layers)
        def _():
            for o in range(1, ne):
                pl.semaphore_signal(z_free, inc=1, device_id={"edge": lax.rem(e + o, ne)}, device_id_type=MESH)

        for k in range(nk):
            for h in range(2):
                rs_pair(k, h).wait_send()
                for o in range(1, nt):
                    rs_cross(k, h, o).wait_send()
                for o in range(1, ne):
                    z_copy(k, h, o).wait_send()
        return 0

    lax.fori_loop(0, layers, layer_step, 0)


def local(edge_feat, edge_counts, reverse, patterns, trip_count, coef, down_weight, up_weight, dense_weight):
    eb, r, de = edge_feat.shape
    nt, ns, ne = lax.axis_size("trip"), lax.axis_size("sub"), lax.axis_size("edge")
    layers, _, ft = down_weight.shape
    _, _, slots, blk, _ = coef.shape
    nk, ranks = r // CHUNK, nt * ns
    edge_rank = lax.axis_index("edge")
    cap = 2 * ((eb // 2 + ne // 2 - 1) // (ne // 2))
    i32 = jnp.int32
    ids = jnp.arange(slots, dtype=i32)
    key = jnp.where(ids < trip_count[0, 0], patterns[0, 0, :, 0], eb)
    before = (key[None, :] < key[:, None]) | ((key[None, :] == key[:, None]) & (ids[None, :] < ids[:, None]))
    rank = jnp.sum(before.astype(i32), axis=1)
    hot = (rank[None, :] == ids[:, None]).astype(i32)
    perm = jnp.sum(hot * ids[None, :], axis=1)
    source = jnp.sum(hot * patterns[0, 0, :, 1][None, :], axis=1)
    first = jnp.sum((key[None, :] < key[:, None]).astype(i32), axis=1)
    same = jnp.sum(hot * (first < rank).astype(i32)[None, :], axis=1)
    cl = jnp.arange(eb, dtype=i32)
    upto = jnp.sum((key[None, :] <= cl[:, None]).astype(i32), axis=1)
    has = jnp.any(key[None, :] == cl[:, None], axis=1).astype(i32)
    last = jnp.maximum(upto - 1, 0)
    mine = lax.dynamic_slice_in_dim(reverse, edge_rank * eb, eb)
    dev = mine // eb
    send_slot = jnp.sum(((dev[:, None] == dev[None, :]) & (cl[None, :] < cl[:, None])).astype(i32), axis=1)
    zslots = jnp.arange(ne * cap, dtype=i32)
    zsrc = jnp.sum(jnp.where(zslots[:, None] == (dev * cap + send_slot)[None, :], cl[None, :], 0), axis=1)
    all_ids = jnp.arange(reverse.shape[0], dtype=i32)
    match = (
        (all_ids[None, :] // eb == dev[:, None])
        & (all_ids[None, :] < mine[:, None])
        & (reverse[None, :] // eb == edge_rank)
    )
    zpos = dev * cap + jnp.sum(match.astype(i32), axis=1)
    tab = jnp.concatenate([perm, source, same, last, has, zsrc, zpos, edge_counts]).astype(i32)

    dims = (nt, ns, ne, eb, r, cap, slots, layers, blk, ft, de)
    vm = pltpu.VMEM
    dma = pltpu.SemaphoreType.DMA
    scratch = [vm((ne * cap, CHUNK, ft // 2), F32) for _ in range(2 * nk)] + [
        vm((slots, blk, blk), F32),
        vm(down_weight.shape, F32),
        vm(up_weight.shape, F32),
        vm(dense_weight.shape, F32),
        vm(down_weight.shape, BF16),
        vm(down_weight.shape, BF16),
        vm(up_weight.shape, BF16),
        vm(up_weight.shape, BF16),
        vm(dense_weight.shape, BF16),
        vm(dense_weight.shape, BF16),
        vm((slots, blk, 3 * blk), BF16),
        vm((eb, 3 * blk, ft), BF16),
        vm((slots + 1, blk, ft), F32),
        vm((ns, nt, eb, r, ft), F32),
        vm((nt, eb, r, ft), F32),
        vm((nt, eb, r, ft), F32),
        vm((eb, r, ft), F32),
        vm((ne * cap, r, ft), F32),
        vm((ranks, eb, r, ft), F32),
        vm((nk, eb * CHUNK, 128), F32),
        dma((6,)),
        dma((2 * nk, nt)),
        dma((2 * nk,)),
        dma((2 * nk, nt)),
        dma((2 * nk, ranks)),
        dma((2 * nk,)),
        dma((2 * nk,)),
        dma((2 * nk, nt)),
        dma((2 * nk, nt)),
        dma((2 * nk, ne)),
        dma((2 * nk, ne)),
        pltpu.SemaphoreType.REGULAR,
    ]
    anywhere = pl.BlockSpec(memory_space=pl.ANY)
    unscaled = pl.pallas_call(
        functools.partial(kernel, dims),
        out_shape=jax.ShapeDtypeStruct(edge_feat.shape, F32),
        in_specs=[pl.BlockSpec(memory_space=pltpu.SMEM)] + [anywhere] * 5,
        out_specs=pl.BlockSpec(memory_space=pltpu.VMEM),
        scratch_shapes=scratch,
        compiler_params=pltpu.CompilerParams(collective_id=0, has_side_effects=True, vmem_limit_bytes=64 * 1024 * 1024 - 65536),
    )(tab, edge_feat, coef[0, 0], down_weight, up_weight, dense_weight)
    return unscaled * INV_TWO


def solution(mesh):
    placed = (
        P(("groups", "edge"), ("trip", "sub"), None),
        P(("groups", "edge")),
        P("groups"),
        P(("groups", "edge"), ("trip", "sub"), None, None),
        P(("groups", "edge"), ("trip", "sub")),
        P(("groups", "edge"), ("trip", "sub"), None, None, None),
        P(),
        P(),
        P(),
    )
    return jax.shard_map(
        local,
        mesh=mesh,
        in_specs=placed,
        out_specs=P(("groups", "edge"), ("trip", "sub"), None),
        check_vma=False,
    )
```
